512 devices in a mesh: section: 2 (over core), tensor: 32 (over z, x), dp: 8 (over y).
Axes of the slice: x: 4, y: 8, z: 8, core: 2. Of those that a mesh axis runs over, the one named last changes fastest.
Arguments:
- grad_out: bfloat16 [2048, 6144], P('dp', 'tensor'), may hold values from -6 to 6
- queries: bfloat16 [2, 2048, 4096], P('section', 'dp', 'tensor'), may hold values from -40 to 40
- key_rows: bfloat16 [2, 2048, 4096], P('section', 'dp', 'tensor'), may hold values from -40 to 40
- value_rows: bfloat16 [2, 2048, 4096], P('section', 'dp', 'tensor'), may hold values from -6 to 6
- w_qkv: bfloat16 [2, 6144, 12288], P('section', 'dp', 'tensor'), may hold values from -0.078125 to 0.078125
- w_out: bfloat16 [2, 4096, 6144], P('section', 'tensor', 'dp'), may hold values from -0.09375 to 0.09375
- seg_lengths: int32 [8, 3], P('dp'), may hold values from 0 to 128, as said below
Outputs:
- input_grad: bfloat16 [2, 2048, 6144], P('section', 'dp', 'tensor')
- out_weight_grad: bfloat16 [2, 4096, 6144], P('section', 'tensor', 'dp')
The draws below stay inside these ranges and needn't reach their ends.
Inputs may be any that keep to these rules, and one draw needn't show every extreme that they name: `seg_lengths`: each row sums to 256, holds one image of exactly 128 patches and either a second of 128 patches and an empty last slot, or two of 64 patches.
All inputs are finite; a program needn't handle non-finite values.
Results may differ from the reference program's by a relative error of at most 0.023.
Values may be sent and summed in bfloat16 or wider, within the bound.
A program may use at most 64 MiB of HBM per device.

```python
import jax
import jax.numpy as jnp
from jax import lax

D = 6144
HD = 128
PACK = 256
MB = 1
SECTIONS = 2
HEADS = 32
PACKS = 8
TOKENS = 2048
N_DP = 8


def query_key(key):
    shape = (SECTIONS, TOKENS, HEADS, HD)
    first = jax.random.normal(jax.random.fold_in(key, 101), shape, jnp.float32)
    second = jax.random.normal(jax.random.fold_in(key, 102), shape, jnp.float32)
    return (first.reshape(SECTIONS, TOKENS, HEADS * HD), second.reshape(SECTIONS, TOKENS, HEADS * HD))


def draw_queries(key, part):
    return query_key(key)[0].astype(jnp.bfloat16)


def draw_key_rows(key, part):
    return query_key(key)[1].astype(jnp.bfloat16)


def draw_seg_lengths(key, part):
    picked = jax.random.randint(jax.random.fold_in(key, 201), (PACKS,), 0, 4)
    larger = PACK // 2
    smaller = PACK // 4
    table = jnp.array([[larger, larger, 0], [larger, smaller, smaller], [smaller, larger, smaller], [smaller, smaller, larger]], jnp.int32)
    return table[picked]


def steps_of(rng, extent, cuts, low, largest):
    gain, own = 1.0, jax.random.fold_in(rng, 6)
    for axis_at, blocks in cuts:
        heights = jnp.exp(jax.random.uniform(jax.random.fold_in(own, axis_at), (blocks,), jnp.float32, low / len(cuts), largest / len(cuts)))
        gain = gain * jnp.repeat(heights, extent[axis_at] // blocks).reshape([-1 if axis == axis_at else 1 for axis in range(len(extent))])
    return gain


def scatter_about(stream_key, shape, deviation, most, split=(), kind=jnp.bfloat16):
    values = jax.random.normal(stream_key, shape, jnp.float32) * deviation
    if len(split) > 0:
        values = steps_of(stream_key, shape, split, -0.22, 0.18) * values
    return jnp.clip(values, min=-most, max=most).astype(kind)


def setup_inputs(seed: int = 0) -> dict:
    splits = jax.random.split(jax.random.key(seed), 8)
    return {
        "grad_out": scatter_about(splits[0], (TOKENS, D), 1.0, 6.0, ((0, 8), (1, 32))),
        "queries": draw_queries(jax.random.fold_in(splits[7], 71), 0),
        "key_rows": draw_key_rows(jax.random.fold_in(splits[7], 71), 0),
        "value_rows": scatter_about(splits[3], (SECTIONS, TOKENS, HEADS * HD), 1.0, 6.0, ((0, 2), (1, 8), (2, 32))),
        "w_qkv": scatter_about(splits[4], (SECTIONS, D, HEADS * 3 * HD), D ** -0.5, 0.078125, ((0, 2), (1, 8), (2, 32))),
        "w_out": scatter_about(splits[5], (SECTIONS, HEADS * HD, D), (HEADS * HD) ** -0.5, 0.09375, ((0, 2), (1, 32), (2, 8))),
        "seg_lengths": draw_seg_lengths(jax.random.fold_in(splits[7], 71), 0),
    }


negative_big = -1e30


def attend_back(query_blk, key_blk, value_blk, grad_attn, same_seg, scaling):
    query_f = query_blk.astype(jnp.float32)
    key_f = key_blk.astype(jnp.float32)
    value_f = value_blk.astype(jnp.float32)
    grad_f = grad_attn.astype(jnp.float32)
    scores = jnp.einsum("hid,hjd->hij", query_f, key_f) * scaling
    scores = jnp.where(same_seg[None], scores, negative_big)
    peak = jnp.max(scores, axis=-1, keepdims=True)
    shifted = jnp.exp(scores - peak)
    probs = shifted / jnp.sum(shifted, axis=-1, keepdims=True)
    probs_low = probs.astype(jnp.bfloat16)
    probs_back = probs_low.astype(jnp.float32)
    attended = jnp.einsum("hij,hjd->hid", probs_back, value_f).astype(jnp.bfloat16)
    grad_value = jnp.einsum("hij,hid->hjd", probs_back, grad_f).astype(jnp.bfloat16)
    grad_probs = jnp.einsum("hid,hjd->hij", grad_f, value_f)
    centred = jnp.sum(probs * grad_probs, axis=-1, keepdims=True)
    grad_scores = (probs * (grad_probs - centred) * scaling).astype(jnp.bfloat16).astype(jnp.float32)
    grad_query = jnp.einsum("hij,hjd->hid", grad_scores, key_f).astype(jnp.bfloat16)
    grad_key = jnp.einsum("hij,hid->hjd", grad_scores, query_f).astype(jnp.bfloat16)
    return attended, grad_query, grad_key, grad_value


def section_back(upstream, queries, key_rows, value_rows, w_qkv, w_out, same_seg):
    scaling = HD ** -0.5
    grad_attn = jnp.dot(upstream, w_out.T, preferred_element_type=jnp.float32).astype(jnp.bfloat16)

    def to_packs(whole):
        return whole.reshape(PACKS, PACK, HEADS, HD).transpose(0, 2, 1, 3)

    def flatten(packed):
        return packed.transpose(0, 2, 1, 3).reshape(TOKENS, HEADS, HD)

    def one_pack(pieces):
        query_blk, key_blk, value_blk, grad_blk, mask_blk = pieces
        return attend_back(query_blk, key_blk, value_blk, grad_blk, mask_blk, scaling)

    attended, grad_query, grad_key, grad_value = lax.map(
        one_pack, (to_packs(queries), to_packs(key_rows), to_packs(value_rows), to_packs(grad_attn), same_seg))
    combined = jnp.stack([flatten(grad_query), flatten(grad_key), flatten(grad_value)], axis=2)
    combined = combined.reshape(TOKENS, HEADS, 3 * HD).transpose(1, 0, 2)
    head_weights = w_qkv.reshape(D, HEADS, 3 * HD).transpose(1, 0, 2)

    def add_head(totals, pieces):
        row_block, col_block = pieces
        head_term = jnp.dot(row_block, col_block.T, preferred_element_type=jnp.float32).astype(jnp.bfloat16)
        head_term = lax.optimization_barrier(head_term)
        return totals + head_term.astype(jnp.float32), None

    branch, _ = lax.scan(add_head, jnp.zeros((TOKENS, D), jnp.float32), (combined, head_weights))
    input_grad = (upstream.astype(jnp.float32) + branch).astype(jnp.bfloat16)
    outputs = flatten(attended).reshape(N_DP, MB * PACK, HEADS * HD)
    grads = upstream.reshape(N_DP, MB * PACK, D)

    def add_replica(totals, pieces):
        row_block, col_block = pieces
        replica_term = jnp.dot(row_block.T, col_block, preferred_element_type=jnp.float32).astype(jnp.bfloat16)
        replica_term = lax.optimization_barrier(replica_term)
        return totals + replica_term.astype(jnp.float32), None

    weight_grad, _ = lax.scan(add_replica, jnp.zeros((HEADS * HD, D), jnp.float32), (outputs, grads))
    return input_grad, weight_grad.astype(jnp.bfloat16)


def reference(grad_out, queries, key_rows, value_rows, w_qkv, w_out, seg_lengths):
    seg_ends = jnp.cumsum(seg_lengths, axis=1).astype(jnp.int32)
    position = jnp.arange(PACK, dtype=jnp.int32)
    seg_ids = jnp.sum((position[None, :, None] >= seg_ends[:, None, :]).astype(jnp.int32), axis=2)
    same_seg = seg_ids[:, :, None] == seg_ids[:, None, :]
    upstream = grad_out
    input_list = [None] * SECTIONS
    weight_list = [None] * SECTIONS
    for section_index in range(SECTIONS - 1, -1, -1):
        input_grad, weight_grad = section_back(upstream, queries[section_index], key_rows[section_index],
                                             value_rows[section_index], w_qkv[section_index], w_out[section_index], same_seg)
        input_list[section_index] = input_grad
        weight_list[section_index] = weight_grad
        upstream = input_grad
    return jnp.stack(input_list), jnp.stack(weight_list)
```

```python
import jax
import jax.numpy as jnp
from jax import lax
from jax.experimental import pallas as pl
from jax.experimental.pallas import tpu as pltpu
from jax.sharding import PartitionSpec as P

MESH = pl.DeviceIdType.MESH
NX, NZ, NY = 4, 8, 8
TOK, HD, COLS = 256, 128, 192
WIDE = NX * COLS
RING = (1, 7, 2, 6, 3, 5, 4)
negative_big = -1e30
F32, BF16 = jnp.float32, jnp.bfloat16


def dot_nt(left, right):
    return lax.dot_general(left, right, (((1,), (1,)), ((), ())), preferred_element_type=F32)


def dot_nn(left, right):
    return lax.dot_general(left, right, (((1,), (0,)), ((), ())), preferred_element_type=F32)


def kernel(seg_ref, up_in, q_ref, k_ref, v_ref, wq_ref, wo_ref, og_ref, ow_ref,
           up, wo, wq, ht, rs1, snd2, rs2, zs, rz, gs, gr, comb, att, hop, fin,
           agz_s, agz_r, agx_s, agx_r, wo_s, wo_r, wq_s, wq_r, rs1_s, rs1_r, rs2_s, rs2_r,
           rz_s, rz_r, g_s, g_r, hop_s, hop_r, gate):
    s = lax.axis_index("section")
    t = lax.axis_index("tensor")
    y = lax.axis_index("dp")
    z, x = t // NX, t % NX
    flip, mirror, across = x + 1 - 2 * (x % 2), NX - 1 - x, (x + 2) % NX

    def pair(k):
        return (flip, mirror) if k % 2 == 0 else (mirror, flip)

    def row(value):
        return {"tensor": z * NX + value}

    def column(value):
        return {"tensor": value * NX + x}

    def ring(value):
        return {"dp": value}

    def copy(src, dst, ss, rs, dev):
        return pltpu.make_async_remote_copy(src_ref=src, dst_ref=dst, send_sem=ss, recv_sem=rs,
                                            device_id=dev, device_id_type=MESH)

    def arrived(dst, rs):
        copy(dst, dst, hop_s.at[0], rs, {"section": 1 - s}).wait_recv()

    barrier = pltpu.get_barrier_semaphore()
    peers = [row(flip), row(mirror), {"section": 1 - s}]
    peers += [column((z + k) % NZ) for k in range(1, NZ)]
    peers += [ring((y + k) % NY) for k in range(1, NY)]
    for peer in peers:
        pl.semaphore_signal(barrier, inc=1, device_id=peer, device_id_type=MESH)
    pl.semaphore_wait(barrier, len(peers))

    def ag_z(src, k):
        return copy(src, up.at[z, x], agz_s.at[k], agz_r.at[k], column((z + k) % NZ))

    def ag_x(src, k):
        zk = (z + NZ - k) % NZ
        own = src if k == 0 else up.at[zk, x]
        near, far = pair(k)
        return (copy(own, up.at[zk, x], agx_s.at[0, k], agx_r.at[0, k], row(near)),
                copy(own, up.at[zk, x], agx_s.at[1, k], agx_r.at[1, k], row(far)),
                copy(up.at[zk, near], up.at[zk, near], agx_s.at[2, k], agx_r.at[2, k], row(far)))

    def take_z(src, k):
        if k:
            arrived(up.at[(z + NZ - k) % NZ, x], agz_r.at[k])
        for each in ag_x(src, k)[:2]:
            each.start()

    def relay_x(src, k):
        arrived(up.at[(z + NZ - k) % NZ, pair(k)[0]], agx_r.at[0, k])
        ag_x(src, k)[2].start()

    def finish_x(k):
        zk = (z + NZ - k) % NZ
        arrived(up.at[zk, pair(k)[1]], agx_r.at[1, k])
        arrived(up.at[zk, across], agx_r.at[2, k])

    def hops(own, full, half, ss, rs, way, step):
        toward = (y + 1) % NY if way == 0 else (y + NY - 1) % NY
        block = (y + NY - step) % NY if way == 0 else (y + step) % NY
        src, dst = (own if step == 0 else full.at[block]), full.at[block]
        if step == 3:
            part = pl.ds(half * way, half)
            src, dst = full.at[block, part], full.at[block, part]
        return copy(src, dst, ss.at[way, step], rs.at[way, step], ring(toward))

    def ring_wait(full, half, rs, way, step):
        block = (y + NY - step - 1) % NY if way == 0 else (y + step + 1) % NY
        ref = full.at[block, pl.ds(half * way, half)] if step == 3 else full.at[block]
        arrived(ref, rs.at[way, step])

    def wo_hop(step, way):
        return hops(wo_ref.at[0], wo, HD // 2, wo_s, wo_r, way, step)

    def wq_hop(step, way):
        return hops(wq_ref.at[0], wq, WIDE // 2, wq_s, wq_r, way, step)

    def wo_step(step):
        for way in (0, 1):
            if step:
                ring_wait(wo, HD // 2, wo_r, way, step - 1)
            if step < 4:
                wo_hop(step, way).start()

    def wq_step(step):
        for way in (0, 1):
            if step:
                ring_wait(wq, WIDE // 2, wq_r, way, step - 1)
            if step < 4:
                wq_hop(step, way).start()

    def early(src):
        for k in RING:
            ag_z(src, k).start()
        wo_step(0)
        take_z(src, 0)
        take_z(src, 1)
        take_z(src, 7)
        relay_x(src, 0)
        wo_step(1)
        take_z(src, 2)
        take_z(src, 6)
        relay_x(src, 1)
        relay_x(src, 7)
        wo_step(2)
        take_z(src, 3)
        take_z(src, 5)
        relay_x(src, 2)
        relay_x(src, 6)
        wo_step(3)
        wq_step(0)
        take_z(src, 4)
        for k in (3, 5, 4):
            relay_x(src, k)
        wo_step(4)
        for k in range(NZ):
            finish_x(k)
        up[z, x] = src[...]
        wq_step(1)

    def late(src):
        pl.semaphore_wait(gate, 1)
        for step in range(5):
            wo_step(step)
            wq_step(step)
        arrived(hop, hop_r.at[0])
        for k in RING:
            ag_z(src, k).start()
        order = (0,) + RING
        for place, k in enumerate(order):
            take_z(src, k)
            if place:
                relay_x(src, order[place - 1])
        relay_x(src, order[-1])
        for k in range(NZ):
            finish_x(k)
        up[z, x] = src[...]

    wo[y] = wo_ref[0]
    wq[y] = wq_ref[0]

    @pl.when(s == 1)
    def _():
        early(up_in)

    @pl.when(s == 0)
    def _():
        late(hop)

    scaling = HD ** -0.5
    grad_t = jnp.zeros((HD, TOK), F32)
    for j in range(NZ):
        grad_t = grad_t + dot_nn(wo[j], up[j].reshape(WIDE, TOK))
    grad_attn = grad_t.T.astype(BF16)
    end0 = seg_ref[0, 0]
    end1 = end0 + seg_ref[0, 1]
    end2 = end1 + seg_ref[0, 2]

    def seg_of(axis):
        place = lax.broadcasted_iota(jnp.int32, (TOK, TOK), axis)
        return (jnp.where(place >= end0, 1, 0) + jnp.where(place >= end1, 1, 0)
                + jnp.where(place >= end2, 1, 0))

    q, k, v = q_ref[0], k_ref[0], v_ref[0]
    scores = jnp.where(seg_of(0) == seg_of(1), dot_nt(q, k) * scaling, negative_big)
    shifted = jnp.exp(scores - jnp.max(scores, axis=1, keepdims=True))
    probs = shifted / jnp.sum(shifted, axis=1, keepdims=True)
    att[...] = dot_nn(probs.astype(BF16), v).T.astype(BF16)
    comb[:, 2 * HD:] = dot_nn(probs.T.astype(BF16), grad_attn).astype(BF16)
    grad_probs = dot_nt(grad_attn, v)
    centred = jnp.sum(probs * grad_probs, axis=1, keepdims=True)
    grad_scores = probs * (grad_probs - centred) * scaling
    comb[:, :HD] = dot_nn(grad_scores.astype(BF16), k).astype(BF16)
    comb[:, HD:2 * HD] = dot_nn(grad_scores.T.astype(BF16), q).astype(BF16)

    def grad_copy(m):
        return copy(gs.at[m], gr.at[m], g_s.at[m], g_r.at[m], ring((y + m) % NY))

    def weight_grad():
        def one(m, _):
            j = (y + m) % NY
            gs[m] = dot_nt(att[...], up[j].reshape(WIDE, TOK)).astype(BF16)

            @pl.when(m > 0)
            def _():
                grad_copy(m).start()
            return 0

        lax.fori_loop(0, NY, one, 0)

    def x_copies(m):
        j = (y + m) % NY
        near, far = pair(m)
        return (copy(ht.at[j, across], rs1.at[m, 1], rs1_s.at[1, m], rs1_r.at[1, m], row(near)),
                copy(ht.at[j, near], rs1.at[m, 0], rs1_s.at[0, m], rs1_r.at[0, m], row(near)),
                copy(snd2.at[m], rs2.at[m], rs2_s.at[m], rs2_r.at[m], row(far)))

    def z_copy(m):
        return copy(zs.at[m], rz.at[z], rz_s.at[m], rz_r.at[z], column((y + m) % NY))

    def term(m):
        j = (y + m) % NY

        def one(i, _):
            ht[j, i] = dot_nt(wq[j, pl.ds(pl.multiple_of(i * COLS, COLS), COLS)], comb[...]).astype(BF16)
            return 0

        lax.fori_loop(0, NX, one, 0)
        for each in x_copies(m)[:2]:
            each.start()

    def second(m):
        j = (y + m) % NY
        arrived(rs1.at[m, 1], rs1_r.at[1, m])
        snd2[m] = (ht[j, pair(m)[1]].astype(F32) + rs1[m, 1].astype(F32)).astype(BF16)
        x_copies(m)[2].start()

    def third(m):
        j = (y + m) % NY
        arrived(rs1.at[m, 0], rs1_r.at[0, m])
        arrived(rs2.at[m], rs2_r.at[m])
        total = ht[j, x].astype(F32) + rs1[m, 0].astype(F32) + rs2[m].astype(F32)
        zs[m] = total.astype(BF16)

        @pl.when(j != z)
        def _():
            z_copy(m).start()

        @pl.when(j == z)
        def _():
            fin[...] = total

    def at_section(which, step, *args):
        @pl.when(s == which)
        def _():
            step(*args)

    at_section(1, wq_step, 2)
    at_section(0, weight_grad)
    order = (0,) + RING
    for place, m in enumerate(order):
        if place == 3:
            at_section(1, wq_step, 3)
        if place == 5:
            at_section(1, wq_step, 4)
        term(m)
        if place >= 1:
            second(order[place - 1])
        if place >= 2:
            third(order[place - 2])

    @pl.when(s == 1)
    def _():
        pl.semaphore_signal(gate, inc=1, device_id={"section": 0}, device_id_type=MESH)

    second(order[-1])
    third(order[-2])
    third(order[-1])
    total = fin[...] + up[z, x].astype(F32)
    for k in RING:
        src = (z + k) % NZ
        arrived(rz.at[src], rz_r.at[src])
        total = total + rz[src].astype(F32)
    og_ref[...] = total.astype(BF16)

    @pl.when(s == 1)
    def _():
        copy(og_ref, hop, hop_s.at[0], hop_r.at[0], {"section": 0}).start()
        weight_grad()

    summed = gs[0].astype(F32)
    for m in range(1, NY):
        arrived(gr.at[m], g_r.at[m])
        summed = summed + gr[m].astype(F32)
    ow_ref[...] = summed.astype(BF16)

    for k in RING:
        ag_z(up_in, k).wait_send()
        grad_copy(k).wait_send()
    for k in range(NZ):
        for each in ag_x(up_in, k) + x_copies(k):
            each.wait_send()

        @pl.when((y + k) % NY != z)
        def _():
            z_copy(k).wait_send()
    for step in range(4):
        for way in (0, 1):
            wo_hop(step, way).wait_send()
            wq_hop(step, way).wait_send()

    @pl.when(s == 1)
    def _():
        copy(og_ref, hop, hop_s.at[0], hop_r.at[0], {"section": 0}).wait_send()


def per_device(grad_out, queries, key_rows, value_rows, w_qkv, w_out, seg_lengths):
    vmem = pl.BlockSpec(memory_space=pltpu.VMEM)
    dma = pltpu.SemaphoreType.DMA
    piece = (COLS, TOK)
    grad, weight = pl.pallas_call(
        kernel,
        out_shape=(jax.ShapeDtypeStruct(piece, BF16), jax.ShapeDtypeStruct((HD, WIDE), BF16)),
        in_specs=[pl.BlockSpec(memory_space=pltpu.SMEM)] + [vmem] * 6,
        out_specs=(vmem, vmem),
        scratch_shapes=[
            pltpu.VMEM((NZ, NX) + piece, BF16),
            pltpu.VMEM((NY, HD, WIDE), BF16),
            pltpu.VMEM((NY, WIDE, 3 * HD), BF16),
            pltpu.VMEM((NZ, NX) + piece, BF16),
            pltpu.VMEM((NZ, 2) + piece, BF16),
            pltpu.VMEM((NZ,) + piece, BF16),
            pltpu.VMEM((NZ,) + piece, BF16),
            pltpu.VMEM((NZ,) + piece, BF16),
            pltpu.VMEM((NZ,) + piece, BF16),
            pltpu.VMEM((NY, HD, WIDE), BF16),
            pltpu.VMEM((NY, HD, WIDE), BF16),
            pltpu.VMEM((TOK, 3 * HD), BF16),
            pltpu.VMEM((HD, TOK), BF16),
            pltpu.VMEM(piece, BF16),
            pltpu.VMEM(piece, F32),
            dma((NZ,)), dma((NZ,)), dma((3, NZ)), dma((3, NZ)),
            dma((2, 4)), dma((2, 4)), dma((2, 4)), dma((2, 4)),
            dma((2, NZ)), dma((2, NZ)), dma((NZ,)), dma((NZ,)),
            dma((NZ,)), dma((NZ,)), dma((NY,)), dma((NY,)), dma((1,)), dma((1,)),
            pltpu.SemaphoreType.REGULAR,
        ],
        compiler_params=pltpu.CompilerParams(collective_id=0, has_side_effects=True),
    )(seg_lengths, grad_out.T, queries, key_rows, value_rows, w_qkv, w_out)
    return grad.T[None], weight[None]


def solution(mesh):
    return jax.shard_map(
        per_device,
        mesh=mesh,
        in_specs=(
            P("dp", "tensor"),
            P("section", "dp", "tensor"),
            P("section", "dp", "tensor"),
            P("section", "dp", "tensor"),
            P("section", "dp", "tensor"),
            P("section", "tensor", "dp"),
            P("dp", None),
        ),
        out_specs=(P("section", "dp", "tensor"), P("section", "tensor", "dp")),
        check_vma=False,
    )
```

```python
import jax
import jax.numpy as jnp
from jax import lax
from jax.experimental import pallas as pl
from jax.experimental.pallas import tpu as pltpu
from jax.sharding import PartitionSpec as P

MESH = pl.DeviceIdType.MESH
NX, NZ, NY = 4, 8, 8
TOK, HD, COLS = 256, 128, 192
WIDE = NX * COLS
RING = (1, 7, 2, 6, 3, 5, 4)
FAR = (4, 3, 5, 2, 6, 1, 7)
LAGS = (3, 6)
CHUNK = 256
negative_big = -1e30
F32, BF16 = jnp.float32, jnp.bfloat16


def dot_nt(left, right):
    return lax.dot_general(left, right, (((1,), (1,)), ((), ())), preferred_element_type=F32)


def dot_nn(left, right):
    return lax.dot_general(left, right, (((1,), (0,)), ((), ())), preferred_element_type=F32)


def kernel(seg_ref, up_in, q_ref, k_ref, v_ref, wq_ref, wo_ref, og_ref, ow_ref,
           up, wo, wq, ht, rs1, snd2, rs2, zs, rz, gs, gr, comb, att, low, prob, hop, fin,
           agz_s, agz_r, agx_s, agx_r, wo_s, wo_r, wq_s, wq_r, rs1_s, rs1_r, rs2_s, rs2_r,
           rz_s, rz_r, g_s, g_r, hop_s, hop_r, gate):
    s = lax.axis_index("section")
    t = lax.axis_index("tensor")
    y = lax.axis_index("dp")
    z, x = t // NX, t % NX
    flip, mirror, across = x + 1 - 2 * (x % 2), NX - 1 - x, (x + 2) % NX

    def pair(k):
        return (flip, mirror) if k % 2 == 0 else (mirror, flip)

    def row(value):
        return {"tensor": z * NX + value}

    def column(value):
        return {"tensor": value * NX + x}

    def ring(value):
        return {"dp": value}

    def copy(src, dst, ss, rs, dev):
        return pltpu.make_async_remote_copy(src_ref=src, dst_ref=dst, send_sem=ss, recv_sem=rs,
                                            device_id=dev, device_id_type=MESH)

    def arrived(dst, rs):
        copy(dst, dst, hop_s.at[0], rs, {"section": 1 - s}).wait_recv()

    barrier = pltpu.get_barrier_semaphore()
    peers = [row(flip), row(mirror), {"section": 1 - s}]
    peers += [column((z + k) % NZ) for k in range(1, NZ)]
    peers += [ring((y + k) % NY) for k in range(1, NY)]
    for peer in peers:
        pl.semaphore_signal(barrier, inc=1, device_id=peer, device_id_type=MESH)
    pl.semaphore_wait(barrier, len(peers))

    def ag_z(src, k):
        return copy(src, up.at[z, x], agz_s.at[k], agz_r.at[k], column((z + k) % NZ))

    def ag_x(src, k):
        zk = (z + NZ - k) % NZ
        own = src if k == 0 else up.at[zk, x]
        near, far = pair(k)
        return (copy(own, up.at[zk, x], agx_s.at[0, k], agx_r.at[0, k], row(near)),
                copy(own, up.at[zk, x], agx_s.at[1, k], agx_r.at[1, k], row(far)),
                copy(up.at[zk, near], up.at[zk, near], agx_s.at[2, k], agx_r.at[2, k], row(far)))

    def take_z(src, k):
        if k:
            arrived(up.at[(z + NZ - k) % NZ, x], agz_r.at[k])
        for each in ag_x(src, k)[:2]:
            each.start()

    def relay_x(src, k):
        arrived(up.at[(z + NZ - k) % NZ, pair(k)[0]], agx_r.at[0, k])
        ag_x(src, k)[2].start()

    def finish_x(k):
        zk = (z + NZ - k) % NZ
        arrived(up.at[zk, pair(k)[1]], agx_r.at[1, k])
        arrived(up.at[zk, across], agx_r.at[2, k])

    streams = [(wo_ref, wo, 0, HD, wo_s, wo_r)]
    for part in range(WIDE // CHUNK):
        streams.append((wq_ref, wq, part * CHUNK, CHUNK, wq_s.at[part], wq_r.at[part]))

    def rows_of(stream, step, way):
        low_row, size = stream[2], stream[3]
        if step == 3:
            low_row, size = low_row + size // 2 * way, size // 2
        return pl.ds(low_row, size)

    def ring_hop(stream, step, way):
        own, full, _, _, ss, rs = stream
        toward = (y + 1) % NY if way == 0 else (y + NY - 1) % NY
        block = (y + NY - step) % NY if way == 0 else (y + step) % NY
        part = rows_of(stream, step, way)
        dst = full.at[block, part]
        src = own.at[0, part] if step == 0 else dst
        return copy(src, dst, ss.at[way, step], rs.at[way, step], ring(toward))

    def ring_step(index, step):
        stream = streams[index]
        for way in (0, 1):
            if step:
                block = (y + NY - step) % NY if way == 0 else (y + step) % NY
                arrived(stream[1].at[block, rows_of(stream, step - 1, way)], stream[5].at[way, step - 1])
            if step < 4:
                ring_hop(stream, step, way).start()

    def parts_step(step):
        for index in (1, 2, 3):
            ring_step(index, step)

    def early(src):
        for k in FAR:
            ag_z(src, k).start()
        ring_step(0, 0)
        ring_step(1, 0)
        take_z(src, 0)
        softmax()
        ring_step(0, 1)
        ring_step(2, 0)
        relay_x(src, 0)
        for place, k in enumerate(FAR):
            take_z(src, k)
            if place >= 1:
                relay_x(src, FAR[place - 1])
            if place == 1:
                ring_step(0, 2)
                ring_step(3, 0)
            if place == 3:
                ring_step(0, 3)
                ring_step(1, 1)
            if place == 5:
                ring_step(2, 1)
        relay_x(src, FAR[-1])
        ring_step(3, 1)
        ring_step(0, 4)
        up[z, x] = src[...]

    def late(src):
        softmax()
        pl.semaphore_wait(gate, 1)
        for step in range(5):
            ring_step(0, step)
            parts_step(step)
        arrived(hop, hop_r.at[0])
        for k in FAR:
            ag_z(src, k).start()
        take_z(src, 0)
        relay_x(src, 0)
        for place, k in enumerate(FAR):
            take_z(src, k)
            if place >= 1:
                relay_x(src, FAR[place - 1])
        relay_x(src, FAR[-1])
        up[z, x] = src[...]

    scaling = HD ** -0.5
    end0 = seg_ref[0, 0]
    end1 = end0 + seg_ref[0, 1]
    end2 = end1 + seg_ref[0, 2]

    def seg_of(axis):
        place = lax.broadcasted_iota(jnp.int32, (TOK, TOK), axis)
        return (jnp.where(place >= end0, 1, 0) + jnp.where(place >= end1, 1, 0)
                + jnp.where(place >= end2, 1, 0))

    def softmax():
        scores = jnp.where(seg_of(0) == seg_of(1), dot_nt(q_ref[0], k_ref[0]) * scaling, negative_big)
        shifted = jnp.exp(scores - jnp.max(scores, axis=1, keepdims=True))
        probs = shifted / jnp.sum(shifted, axis=1, keepdims=True)
        prob[...] = probs
        low[...] = probs.T.astype(BF16)
        att[...] = dot_nn(probs.astype(BF16), v_ref[0]).T.astype(BF16)

    def at_section(which, step, *args):
        @pl.when(s == which)
        def _():
            step(*args)

    wo[y] = wo_ref[0]
    wq[y] = wq_ref[0]

    @pl.when(s == 1)
    def _():
        early(up_in)

    @pl.when(s == 0)
    def _():
        late(hop)

    grad_t = jnp.zeros((HD, TOK), F32)
    for place, k in enumerate((0,) + FAR):
        finish_x(k)
        zk = (z + NZ - k) % NZ
        grad_t = grad_t + dot_nn(wo[zk], up[zk].reshape(WIDE, TOK))
        if place in (2, 4, 6):
            at_section(1, ring_step, place // 2, 2)
    grad_attn = grad_t.T.astype(BF16)
    q, k, v = q_ref[0], k_ref[0], v_ref[0]
    probs = prob[...]
    comb[:, 2 * HD:] = dot_nn(low[...], grad_attn).astype(BF16)
    grad_probs = dot_nt(grad_attn, v)
    centred = jnp.sum(probs * grad_probs, axis=1, keepdims=True)
    grad_scores = probs * (grad_probs - centred) * scaling
    comb[:, :HD] = dot_nn(grad_scores.astype(BF16), k).astype(BF16)
    comb[:, HD:2 * HD] = dot_nn(grad_scores.T.astype(BF16), q).astype(BF16)

    def grad_part(block, way):
        return dot_nt(att[...], up[block, pl.ds(2 * way, 2)].reshape(WIDE // 2, TOK))

    def grad_copy(step, way):
        toward = (y + 1) % NY if way == 0 else (y + NY - 1) % NY
        return copy(gs.at[way, step], gr.at[way, step], g_s.at[way, step], g_r.at[way, step], ring(toward))

    def grad_step(step):
        for way in (0, 1):
            if step == NY - 1:
                block = y
            else:
                block = (y + NY - 1 - step) % NY if way == 0 else (y + 1 + step) % NY
            part = grad_part(block, way)
            if step:
                arrived(gr.at[way, step - 1], g_r.at[way, step - 1])
                part = part + gr[way, step - 1].astype(F32)
            if step == NY - 1:
                ow_ref[:, pl.ds(way * WIDE // 2, WIDE // 2)] = part.astype(BF16)
            else:
                gs[way, step] = part.astype(BF16)
                grad_copy(step, way).start()

    base = s * y + (1 - s) * z

    def x_copies(m):
        j = (base + m) % NZ
        near, far = pair(m)
        return (copy(ht.at[j, across], rs1.at[m, 1], rs1_s.at[1, m], rs1_r.at[1, m], row(near)),
                copy(ht.at[j, near], rs1.at[m, 0], rs1_s.at[0, m], rs1_r.at[0, m], row(near)),
                copy(snd2.at[m], rs2.at[m], rs2_s.at[m], rs2_r.at[m], row(far)))

    def z_copy(m):
        return copy(zs.at[m], rz.at[z], rz_s.at[m], rz_r.at[z], column((base + m) % NZ))

    def term(m):
        j = (base + m) % NZ

        def one(i, _):
            ht[j, i] = dot_nt(wq[j, pl.ds(pl.multiple_of(i * COLS, COLS), COLS)], comb[...]).astype(BF16)
            return 0

        lax.fori_loop(0, NX, one, 0)
        for each in x_copies(m)[:2]:
            each.start()

    def second(m):
        j = (base + m) % NZ
        arrived(rs1.at[m, 1], rs1_r.at[1, m])
        snd2[m] = (ht[j, pair(m)[1]].astype(F32) + rs1[m, 1].astype(F32)).astype(BF16)
        x_copies(m)[2].start()

    def third(m):
        j = (base + m) % NZ
        arrived(rs1.at[m, 0], rs1_r.at[0, m])
        arrived(rs2.at[m], rs2_r.at[m])
        total = ht[j, x].astype(F32) + rs1[m, 0].astype(F32) + rs2[m].astype(F32)
        zs[m] = total.astype(BF16)

        @pl.when(j != z)
        def _():
            z_copy(m).start()

        @pl.when(j == z)
        def _():
            fin[...] = total

    def open_gate():
        pl.semaphore_signal(gate, inc=1, device_id={"section": 0}, device_id_type=MESH)

    def scatter(order, first):
        lag2, lag3 = LAGS
        for place in range(NZ + lag3):
            if first and place in (0, 1, 2):
                ring_step(1 + place, 3)
                if place == 2:
                    open_gate()
            if first and place == 5:
                parts_step(4)
            if place < NZ:
                term(order[place])
            if 0 <= place - lag2 < NZ:
                second(order[place - lag2])
            if place >= lag3:
                third(order[place - lag3])
            if not first and place % 2 == 0:
                grad_step(place // 2)

    at_section(1, scatter, (0,) + RING, True)
    at_section(0, scatter, FAR + (0,), False)
    total = fin[...] + up[z, x].astype(F32)
    for k in RING:
        src = (z + k) % NZ
        arrived(rz.at[src], rz_r.at[src])
        total = total + rz[src].astype(F32)
    og_ref[...] = total.astype(BF16)

    @pl.when(s == 1)
    def _():
        copy(og_ref, hop, hop_s.at[0], hop_r.at[0], {"section": 0}).start()
        for step in range(NY - 1):
            grad_step(step)

    grad_step(NY - 1)

    for k in RING:
        ag_z(up_in, k).wait_send()
    for k in range(NZ):
        for each in ag_x(up_in, k) + x_copies(k):
            each.wait_send()

        @pl.when((base + k) % NZ != z)
        def _():
            z_copy(k).wait_send()
    for step in range(4):
        for way in (0, 1):
            for stream in streams:
                ring_hop(stream, step, way).wait_send()
    for step in range(NY - 1):
        for way in (0, 1):
            grad_copy(step, way).wait_send()

    @pl.when(s == 1)
    def _():
        copy(og_ref, hop, hop_s.at[0], hop_r.at[0], {"section": 0}).wait_send()


def per_device(grad_out, queries, key_rows, value_rows, w_qkv, w_out, seg_lengths):
    vmem = pl.BlockSpec(memory_space=pltpu.VMEM)
    dma = pltpu.SemaphoreType.DMA
    piece = (COLS, TOK)
    grad, weight = pl.pallas_call(
        kernel,
        out_shape=(jax.ShapeDtypeStruct(piece, BF16), jax.ShapeDtypeStruct((HD, WIDE), BF16)),
        in_specs=[pl.BlockSpec(memory_space=pltpu.SMEM)] + [vmem] * 6,
        out_specs=(vmem, vmem),
        scratch_shapes=[
            pltpu.VMEM((NZ, NX) + piece, BF16),
            pltpu.VMEM((NY, HD, WIDE), BF16),
            pltpu.VMEM((NY, WIDE, 3 * HD), BF16),
            pltpu.VMEM((NZ, NX) + piece, BF16),
            pltpu.VMEM((NZ, 2) + piece, BF16),
            pltpu.VMEM((NZ,) + piece, BF16),
            pltpu.VMEM((NZ,) + piece, BF16),
            pltpu.VMEM((NZ,) + piece, BF16),
            pltpu.VMEM((NZ,) + piece, BF16),
            pltpu.VMEM((2, NY - 1, HD, WIDE // 2), BF16),
            pltpu.VMEM((2, NY - 1, HD, WIDE // 2), BF16),
            pltpu.VMEM((TOK, 3 * HD), BF16),
            pltpu.VMEM((HD, TOK), BF16),
            pltpu.VMEM((TOK, TOK), BF16),
            pltpu.VMEM((TOK, TOK), F32),
            pltpu.VMEM(piece, BF16),
            pltpu.VMEM(piece, F32),
            dma((NZ,)), dma((NZ,)), dma((3, NZ)), dma((3, NZ)),
            dma((2, 4)), dma((2, 4)), dma((3, 2, 4)), dma((3, 2, 4)),
            dma((2, NZ)), dma((2, NZ)), dma((NZ,)), dma((NZ,)),
            dma((NZ,)), dma((NZ,)), dma((2, NY - 1)), dma((2, NY - 1)), dma((1,)), dma((1,)),
            pltpu.SemaphoreType.REGULAR,
        ],
        compiler_params=pltpu.CompilerParams(collective_id=0, has_side_effects=True),
    )(seg_lengths, grad_out.T, queries, key_rows, value_rows, w_qkv, w_out)
    return grad.T[None], weight[None]


def solution(mesh):
    return jax.shard_map(
        per_device,
        mesh=mesh,
        in_specs=(
            P("dp", "tensor"),
            P("section", "dp", "tensor"),
            P("section", "dp", "tensor"),
            P("section", "dp", "tensor"),
            P("section", "dp", "tensor"),
            P("section", "tensor", "dp"),
            P("dp", None),
        ),
        out_specs=(P("section", "dp", "tensor"), P("section", "tensor", "dp")),
        check_vma=False,
    )
```

```python
import jax
import jax.numpy as jnp
from jax import lax
from jax.experimental import pallas as pl
from jax.experimental.pallas import tpu as pltpu
from jax.sharding import PartitionSpec as P

MESH = pl.DeviceIdType.MESH
NX, NZ, NY = 4, 8, 8
TOK, HD, COLS = 256, 128, 192
WIDE = NX * COLS
RING = (1, 7, 2, 6, 3, 5, 4)
FAR = (4, 3, 5, 2, 6, 1, 7)
TAKE = (5, 7, 1, 6, 2, 3, 4)
LAGS = (4, 7)
GRAD_AT = {0: 0, 4: 1, 6: 2, 8: 3, 10: 4, 12: 5, 14: 6}
CHUNK = 256
negative_big = -1e30
F32, BF16 = jnp.float32, jnp.bfloat16


def dot_nt(left, right):
    return lax.dot_general(left, right, (((1,), (1,)), ((), ())), preferred_element_type=F32)


def dot_nn(left, right):
    return lax.dot_general(left, right, (((1,), (0,)), ((), ())), preferred_element_type=F32)


def kernel(seg_ref, up_in, q_ref, k_ref, v_ref, wq_ref, wo_ref, og_ref, ow_ref,
           up, wo, wq, ht, rs1, snd2, rs2, zs, rz, gs, gr, comb, att, low, prob, fin,
           agz_s, agz_r, agx_s, agx_r, wo_s, wo_r, wq_s, wq_r, rs1_s, rs1_r, rs2_s, rs2_r,
           rz_s, rz_r, g_s, g_r, hop_s, gate):
    s = lax.axis_index("section")
    t = lax.axis_index("tensor")
    y = lax.axis_index("dp")
    z, x = t // NX, t % NX
    flip, mirror, across = x + 1 - 2 * (x % 2), NX - 1 - x, (x + 2) % NX

    def pair(k):
        return (flip, mirror) if k % 2 == 0 else (mirror, flip)

    def row(value):
        return {"tensor": z * NX + value}

    def column(value):
        return {"tensor": value * NX + x}

    def ring(value):
        return {"dp": value}

    def copy(src, dst, ss, rs, dev):
        return pltpu.make_async_remote_copy(src_ref=src, dst_ref=dst, send_sem=ss, recv_sem=rs,
                                            device_id=dev, device_id_type=MESH)

    def arrived(dst, rs):
        copy(dst, dst, hop_s.at[0], rs, {"section": 1 - s}).wait_recv()

    barrier = pltpu.get_barrier_semaphore()
    peers = [row(flip), row(mirror), {"section": 1 - s}]
    peers += [column((z + k) % NZ) for k in range(1, NZ)]
    peers += [{"section": 1 - s, **column((z + k) % NZ)} for k in TAKE[:-1]]
    peers += [ring((y + k) % NY) for k in (1, NY - 1)]
    for peer in peers:
        pl.semaphore_signal(barrier, inc=1, device_id=peer, device_id_type=MESH)
    pl.semaphore_wait(barrier, len(peers))

    def ag_z(src, k):
        return copy(src, up.at[z, x], agz_s.at[k], agz_r.at[k], column((z + k) % NZ))

    def ag_relay(k):
        zk = (z + 3) % NZ
        return copy(up.at[zk, x], up.at[zk, x], agz_s.at[k], agz_r.at[k], column((z + NZ - 1) % NZ))

    def pass_on(k):
        where = {"section": 0, **column((z + k) % NZ)}
        return copy(og_ref, up.at[z, x], hop_s.at[k], agz_r.at[k], where)

    def ag_x(src, k):
        zk = (z + NZ - k) % NZ
        own = src if k == 0 and src is not None else up.at[zk, x]
        near, far = pair(k)
        return (copy(own, up.at[zk, x], agx_s.at[0, k], agx_r.at[0, k], row(near)),
                copy(own, up.at[zk, x], agx_s.at[1, k], agx_r.at[1, k], row(far)),
                copy(up.at[zk, near], up.at[zk, near], agx_s.at[2, k], agx_r.at[2, k], row(far)))

    def take_z(src, k):
        if k or src is None:
            arrived(up.at[(z + NZ - k) % NZ, x], agz_r.at[k])
        if k == 5:
            ag_relay(4).start()
        for each in ag_x(src, k)[:2]:
            each.start()

    def relay_x(src, k):
        arrived(up.at[(z + NZ - k) % NZ, pair(k)[0]], agx_r.at[0, k])
        ag_x(src, k)[2].start()

    def finish_x(k):
        zk = (z + NZ - k) % NZ
        arrived(up.at[zk, pair(k)[1]], agx_r.at[1, k])
        arrived(up.at[zk, across], agx_r.at[2, k])

    streams = [(wo_ref, wo, 0, HD, wo_s, wo_r)]
    for part in range(WIDE // CHUNK):
        streams.append((wq_ref, wq, part * CHUNK, CHUNK, wq_s.at[part], wq_r.at[part]))

    def rows_of(stream, step, way):
        low_row, size = stream[2], stream[3]
        if step == 3:
            low_row, size = low_row + size // 2 * way, size // 2
        return pl.ds(low_row, size)

    def ring_hop(stream, step, way):
        own, full, _, _, ss, rs = stream
        toward = (y + 1) % NY if way == 0 else (y + NY - 1) % NY
        block = (y + NY - step) % NY if way == 0 else (y + step) % NY
        part = rows_of(stream, step, way)
        dst = full.at[block, part]
        src = own.at[0, part] if step == 0 else dst
        return copy(src, dst, ss.at[way, step], rs.at[way, step], ring(toward))

    def ring_step(index, step):
        stream = streams[index]
        for way in (0, 1):
            if step:
                block = (y + NY - step) % NY if way == 0 else (y + step) % NY
                arrived(stream[1].at[block, rows_of(stream, step - 1, way)], stream[5].at[way, step - 1])
            if step < 4:
                ring_hop(stream, step, way).start()

    def parts_step(step):
        for index in (1, 2, 3):
            ring_step(index, step)

    def gather(src, between):
        take_z(src, 0)
        if src is not None:
            softmax()
        between(-1)
        relay_x(src, 0)
        for place, k in enumerate(TAKE):
            take_z(src, k)
            if place >= 1:
                relay_x(src, TAKE[place - 1])
            between(place)
        relay_x(src, TAKE[-1])

    def early(src):
        for k in TAKE[:-1]:
            ag_z(src, k).start()
        ring_step(0, 0)
        ring_step(1, 0)

        def between(place):
            if place == -1:
                ring_step(0, 1)
                ring_step(2, 0)
            if place == 1:
                ring_step(0, 2)
                ring_step(3, 0)
            if place == 3:
                ring_step(0, 3)
                ring_step(1, 1)
            if place == 5:
                ring_step(2, 1)

        gather(src, between)
        ring_step(3, 1)
        ring_step(0, 4)
        up[z, x] = src[...]

    def late():
        softmax()
        pl.semaphore_wait(gate, 1)
        for step in range(3):
            ring_step(0, step)
            parts_step(step)
        ring_step(0, 3)

        def between(place):
            if place in (1, 3, 5):
                ring_step(1 + place // 2, 3)

        gather(None, between)
        ring_step(0, 4)

    def open_gate():
        pl.semaphore_signal(gate, inc=1, device_id={"section": 0}, device_id_type=MESH)

    scaling = HD ** -0.5
    end0 = seg_ref[0, 0]
    end1 = end0 + seg_ref[0, 1]
    end2 = end1 + seg_ref[0, 2]

    def seg_of(axis):
        place = lax.broadcasted_iota(jnp.int32, (TOK, TOK), axis)
        return (jnp.where(place >= end0, 1, 0) + jnp.where(place >= end1, 1, 0)
                + jnp.where(place >= end2, 1, 0))

    def softmax():
        scores = jnp.where(seg_of(0) == seg_of(1), dot_nt(q_ref[0], k_ref[0]) * scaling, negative_big)
        shifted = jnp.exp(scores - jnp.max(scores, axis=1, keepdims=True))
        probs = shifted / jnp.sum(shifted, axis=1, keepdims=True)
        prob[...] = probs
        low[...] = probs.T.astype(BF16)
        att[...] = dot_nn(probs.astype(BF16), v_ref[0]).T.astype(BF16)

    def at_section(which, step, *args):
        @pl.when(s == which)
        def _():
            step(*args)

    wo[y] = wo_ref[0]
    wq[y] = wq_ref[0]

    @pl.when(s == 1)
    def _():
        early(up_in)

    @pl.when(s == 0)
    def _():
        late()

    grad_t = jnp.zeros((HD, TOK), F32)
    for place, k in enumerate((0,) + TAKE):
        finish_x(k)
        zk = (z + NZ - k) % NZ
        grad_t = grad_t + dot_nn(wo[zk], up[zk].reshape(WIDE, TOK))
        if place in (2, 4, 6):
            at_section(1, ring_step, place // 2, 2)
    grad_attn = grad_t.T.astype(BF16)
    q, k, v = q_ref[0], k_ref[0], v_ref[0]
    probs = prob[...]
    comb[:, 2 * HD:] = dot_nn(low[...], grad_attn).astype(BF16)
    grad_probs = dot_nt(grad_attn, v)
    centred = jnp.sum(probs * grad_probs, axis=1, keepdims=True)
    grad_scores = probs * (grad_probs - centred) * scaling
    comb[:, :HD] = dot_nn(grad_scores.astype(BF16), k).astype(BF16)
    comb[:, HD:2 * HD] = dot_nn(grad_scores.T.astype(BF16), q).astype(BF16)

    def grad_part(block, way):
        return dot_nt(att[...], up[block, pl.ds(2 * way, 2)].reshape(WIDE // 2, TOK))

    def grad_copy(step, way):
        toward = (y + 1) % NY if way == 0 else (y + NY - 1) % NY
        return copy(gs.at[way, step], gr.at[way, step], g_s.at[way, step], g_r.at[way, step], ring(toward))

    def grad_step(step):
        for way in (0, 1):
            if step == NY - 1:
                block = y
            else:
                block = (y + NY - 1 - step) % NY if way == 0 else (y + 1 + step) % NY
            part = grad_part(block, way)
            if step:
                arrived(gr.at[way, step - 1], g_r.at[way, step - 1])
                part = part + gr[way, step - 1].astype(F32)
            if step == NY - 1:
                ow_ref[:, pl.ds(way * WIDE // 2, WIDE // 2)] = part.astype(BF16)
            else:
                gs[way, step] = part.astype(BF16)
                grad_copy(step, way).start()

    base = s * y + (1 - s) * z

    def x_copies(m):
        j = (base + m) % NZ
        near, far = pair(m)
        return (copy(ht.at[j, across], rs1.at[m, 1], rs1_s.at[1, m], rs1_r.at[1, m], row(near)),
                copy(ht.at[j, near], rs1.at[m, 0], rs1_s.at[0, m], rs1_r.at[0, m], row(near)),
                copy(snd2.at[m], rs2.at[m], rs2_s.at[m], rs2_r.at[m], row(far)))

    def z_copy(m):
        return copy(zs.at[m], rz.at[z], rz_s.at[m], rz_r.at[z], column((base + m) % NZ))

    def term(m):
        j = (base + m) % NZ

        def one(i, _):
            ht[j, i] = dot_nt(wq[j, pl.ds(pl.multiple_of(i * COLS, COLS), COLS)], comb[...]).astype(BF16)
            return 0

        lax.fori_loop(0, NX, one, 0)
        for each in x_copies(m)[:2]:
            each.start()

    def second(m):
        j = (base + m) % NZ
        arrived(rs1.at[m, 1], rs1_r.at[1, m])
        snd2[m] = (ht[j, pair(m)[1]].astype(F32) + rs1[m, 1].astype(F32)).astype(BF16)
        x_copies(m)[2].start()

    def third(m):
        j = (base + m) % NZ
        arrived(rs1.at[m, 0], rs1_r.at[0, m])
        arrived(rs2.at[m], rs2_r.at[m])
        total = ht[j, x].astype(F32) + rs1[m, 0].astype(F32) + rs2[m].astype(F32)
        zs[m] = total.astype(BF16)

        @pl.when(j != z)
        def _():
            z_copy(m).start()

        @pl.when(j == z)
        def _():
            fin[...] = total

    def scatter(order, first):
        lag2, lag3 = LAGS
        for place in range(NZ + lag3):
            if first and place in (0, 1, 2):
                ring_step(1 + place, 3)
            if place == (5 if first else 0):
                parts_step(4)
                if first:
                    open_gate()
            if place < NZ:
                term(order[place])
            if 0 <= place - lag2 < NZ:
                second(order[place - lag2])
            if place >= lag3:
                third(order[place - lag3])
            if not first and place in GRAD_AT:
                grad_step(GRAD_AT[place])

    at_section(1, scatter, (0,) + RING, True)
    at_section(0, scatter, FAR + (0,), False)
    total = fin[...] + up[z, x].astype(F32)
    for k in RING:
        src = (z + k) % NZ
        arrived(rz.at[src], rz_r.at[src])
        total = total + rz[src].astype(F32)
    og_ref[...] = total.astype(BF16)

    @pl.when(s == 1)
    def _():
        for k in (0,) + TAKE[:-1]:
            pass_on(k).start()
        for step in range(NY - 1):
            grad_step(step)

    grad_step(NY - 1)

    ag_relay(4).wait_send()
    for k in range(NZ):
        for each in ag_x(up_in, k) + x_copies(k):
            each.wait_send()

        @pl.when((base + k) % NZ != z)
        def _():
            z_copy(k).wait_send()
    for step in range(4):
        for way in (0, 1):
            for stream in streams:
                ring_hop(stream, step, way).wait_send()
    for step in range(NY - 1):
        for way in (0, 1):
            grad_copy(step, way).wait_send()

    @pl.when(s == 1)
    def _():
        for k in TAKE[:-1]:
            ag_z(up_in, k).wait_send()
        for k in (0,) + TAKE[:-1]:
            pass_on(k).wait_send()


def per_device(grad_out, queries, key_rows, value_rows, w_qkv, w_out, seg_lengths):
    vmem = pl.BlockSpec(memory_space=pltpu.VMEM)
    dma = pltpu.SemaphoreType.DMA
    piece = (COLS, TOK)
    grad, weight = pl.pallas_call(
        kernel,
        out_shape=(jax.ShapeDtypeStruct(piece, BF16), jax.ShapeDtypeStruct((HD, WIDE), BF16)),
        in_specs=[pl.BlockSpec(memory_space=pltpu.SMEM)] + [vmem] * 6,
        out_specs=(vmem, vmem),
        scratch_shapes=[
            pltpu.VMEM((NZ, NX) + piece, BF16),
            pltpu.VMEM((NY, HD, WIDE), BF16),
            pltpu.VMEM((NY, WIDE, 3 * HD), BF16),
            pltpu.VMEM((NZ, NX) + piece, BF16),
            pltpu.VMEM((NZ, 2) + piece, BF16),
            pltpu.VMEM((NZ,) + piece, BF16),
            pltpu.VMEM((NZ,) + piece, BF16),
            pltpu.VMEM((NZ,) + piece, BF16),
            pltpu.VMEM((NZ,) + piece, BF16),
            pltpu.VMEM((2, NY - 1, HD, WIDE // 2), BF16),
            pltpu.VMEM((2, NY - 1, HD, WIDE // 2), BF16),
            pltpu.VMEM((TOK, 3 * HD), BF16),
            pltpu.VMEM((HD, TOK), BF16),
            pltpu.VMEM((TOK, TOK), BF16),
            pltpu.VMEM((TOK, TOK), F32),
            pltpu.VMEM(piece, F32),
            dma((NZ,)), dma((NZ,)), dma((3, NZ)), dma((3, NZ)),
            dma((2, 4)), dma((2, 4)), dma((3, 2, 4)), dma((3, 2, 4)),
            dma((2, NZ)), dma((2, NZ)), dma((NZ,)), dma((NZ,)),
            dma((NZ,)), dma((NZ,)), dma((2, NY - 1)), dma((2, NY - 1)), dma((NZ,)),
            pltpu.SemaphoreType.REGULAR,
        ],
        compiler_params=pltpu.CompilerParams(collective_id=0, has_side_effects=True),
    )(seg_lengths, grad_out.T, queries, key_rows, value_rows, w_qkv, w_out)
    return grad.T[None], weight[None]


def solution(mesh):
    return jax.shard_map(
        per_device,
        mesh=mesh,
        in_specs=(
            P("dp", "tensor"),
            P("section", "dp", "tensor"),
            P("section", "dp", "tensor"),
            P("section", "dp", "tensor"),
            P("section", "dp", "tensor"),
            P("section", "tensor", "dp"),
            P("dp", None),
        ),
        out_specs=(P("section", "dp", "tensor"), P("section", "tensor", "dp")),
        check_vma=False,
    )
```
